32 devices in a mesh: row: 8 (over z, x), col: 4 (over y, core).
Axes of the slice: x: 2, y: 2, z: 4, core: 2. Of those that a mesh axis runs over, the one named last changes fastest.
Arguments:
- trailing: float32 [8192, 1536], P('row', 'col'), may hold values from -6 to 6
- reflectors: float32 [8192, 256], P('row', 'col'), may hold values from -6 to 6
- factor: float32 [256, 256], replicated, as said below
- column_sums: float32 [8192, 8], P('row', 'col'), may hold values from -6 to 6
- row_sums: float32 [16, 1536], P('row', 'col'), may hold values from -6 to 6
Outputs:
- updated: float32 [8192, 1536], P('row', 'col')
- column_checks: float32 [8192, 8], P('row', 'col')
- row_checks: float32 [16, 1536], P('row', 'col')
The draws below stay inside these ranges and needn't reach their ends.
Inputs may be any that keep to these rules, and one draw needn't show every extreme that they name: `factor`: zero below the diagonal.
All inputs are finite; a program needn't handle non-finite values.
Results may differ from the reference program's by a relative error of at most 0.000067.
Values sent between devices are 32-bit elements; how exact they have to be, the bound alone decides.
No kernel may reach another device: no remote copies, remote signals or barrier semaphores. Data moves between devices by JAX's collectives and lax.ppermute only.
A program may use at most 64 MiB of HBM per device.

```python
import math
import jax
import jax.numpy as jnp
from jax import lax

NB = 256
CHK = 2
ROWS_DEV = 1024
M = 8192
N = 1536
N_ROW = 8
N_COL = 4


def draw_factor(key, part):
    values = jax.random.normal(key, (NB, NB), jnp.float32) * (1.0 / (NB * math.sqrt(M)))
    rowpos = jnp.arange(NB)[:, None]
    colpos = jnp.arange(NB)[None, :]
    return jnp.where(rowpos <= colpos, values, jnp.float32(0.0))


def steps_of(key, extent, pieces, least, high):
    def one(dim, blocks):
        draws = jax.random.uniform(jax.random.fold_in(jax.random.fold_in(key, 6), dim), (blocks,), jnp.float32, least / len(pieces), high / len(pieces))
        return jnp.repeat(jnp.exp(draws), extent[dim] // blocks).reshape((-1,) + (1,) * (len(extent) - dim - 1))

    factor_of = one(*pieces[0])
    for cut in pieces[1:]:
        factor_of = factor_of * one(*cut)
    return factor_of


def noise(rng, extent, scale, bound, pieces=(), dtype=jnp.bfloat16):
    array = scale * jax.random.normal(rng, extent, jnp.float32)
    if pieces:
        array = array * steps_of(rng, extent, pieces, -0.22, 0.18)
    return jnp.clip(array, -bound, bound).astype(dtype)


def setup_inputs(seed: int = 0) -> dict:
    key_list = jax.random.split(jax.random.key(seed), 6)
    trailing = noise(key_list[0], (M, N), 1.0, 6.0, ((0, 8), (1, 4)), jnp.float32)
    reflectors = noise(key_list[1], (M, NB), 1.0, 6.0, ((0, 8), (1, 4)), jnp.float32)
    factor = draw_factor(jax.random.fold_in(key_list[5], 71), 0)
    column_sums = noise(key_list[3], (M, CHK * N_COL), 1.0, 6.0, ((0, 8), (1, 4)), jnp.float32)
    row_sums = noise(key_list[4], (CHK * N_ROW, N), 1.0, 6.0, ((0, 8), (1, 4)), jnp.float32)
    return {"trailing": trailing, "reflectors": reflectors, "factor": factor, "column_sums": column_sums, "row_sums": row_sums}


def matmul(left, right):
    return jnp.dot(left, right, precision=lax.Precision.HIGHEST, preferred_element_type=jnp.float32)

def reference(trailing, reflectors, factor, column_sums, row_sums):
    product_main = matmul(reflectors.T, trailing)
    product_check = matmul(reflectors.T, column_sums)
    main_image = matmul(factor.T, product_main)
    check_image = matmul(factor.T, product_check)
    updated = trailing - matmul(reflectors, main_image)
    column_checks = column_sums - matmul(reflectors, check_image)
    local = jnp.arange(ROWS_DEV).astype(jnp.float32)
    scale = 1.0 / jnp.sqrt(jnp.float32(ROWS_DEV))
    weights = jnp.stack([jnp.ones((ROWS_DEV,), jnp.float32) * scale, (local + 1.0) * scale / ROWS_DEV])
    blocks = reflectors.reshape(N_ROW, ROWS_DEV, NB)
    coeff = jnp.einsum('cj,pjk->pck', weights, blocks, precision=lax.Precision.HIGHEST)
    coeff = coeff.reshape(CHK * N_ROW, NB)
    row_checks = row_sums - matmul(coeff, main_image)
    return (updated, column_checks, row_checks)
```

```python
import jax
import jax.numpy as jnp
from jax import lax
from jax.sharding import PartitionSpec as P

EXTRA = 8


def dot(left, right, dims=((1,), (0,))):
    return lax.dot_general(left, right, (dims, ((), ())), precision=lax.Precision.HIGH, preferred_element_type=jnp.float32)


def swap(value, axis, size, distance):
    return lax.ppermute(value, axis, [(i, i ^ distance) for i in range(size)])


def xor_blocks(value, dim, blocks, index):
    shape = value.shape
    width = shape[dim] // blocks
    step = 1
    while step < blocks:
        split = shape[:dim] + (blocks // (2 * step), 2, step * width) + shape[dim + 1 :]
        turned = jnp.flip(value.reshape(split), dim + 1).reshape(shape)
        value = jnp.where((index // step) % 2 == 1, turned, value)
        step *= 2
    return value


def check_weights(count):
    local = jnp.arange(count).astype(jnp.float32)
    scale = 1.0 / jnp.sqrt(jnp.float32(count))
    return jnp.stack([jnp.ones((count,), jnp.float32) * scale, (local + 1.0) * scale / count])


def plain(trailing, reflectors, factor, column_sums, row_sums):
    panel = lax.all_gather(reflectors, "col", axis=1, tiled=True)
    columns = trailing.shape[1]
    joined = jnp.concatenate([trailing, column_sums], axis=1)
    image = dot(factor.T, lax.psum(dot(panel.T, joined), "row"))
    joined = joined - dot(panel, image)
    coeff = dot(check_weights(trailing.shape[0]), panel)
    return (joined[:, :columns], joined[:, columns:], row_sums - dot(coeff, image[:, :columns]))


def steps(n_row, n_col, trailing, reflectors, factor, column_sums, row_sums):
    rows, columns = trailing.shape
    width = reflectors.shape[1]
    row = lax.axis_index("row")
    col = lax.axis_index("col")
    side = row % 2
    half = n_col // 4 * width
    sums = column_sums.T
    order = sorted(range(1, n_col), key=lambda s: (s & (s - 1), -s))
    got = {0: reflectors.T}
    for s in order:
        low = s & -s
        got[s] = swap(got[s - low], "col", n_col, low)
    panel = [jnp.concatenate([got[s] for s in range(n_col // 2 * g, n_col // 2 * (g + 1))]) for g in range(2)]
    summed = []
    for g in range(2):
        product = dot(panel[g], trailing)
        check = dot(sums, panel[g], ((1,), (1,)))
        blocks = [
            jnp.concatenate(
                [
                    product[h * half : (h + 1) * half],
                    jnp.pad(check[:, h * half : (h + 1) * half], ((0, EXTRA - check.shape[0]), (0, columns - half))),
                ]
            )
            for h in range(2)
        ]
        keep = jnp.where(side == 0, blocks[0], blocks[1])
        send = jnp.where(side == 0, blocks[1], blocks[0])
        total = keep + swap(send, "row", n_row, 1)
        distance = 2
        while distance < n_row:
            total = total + swap(total, "row", n_row, distance)
            distance *= 2
        summed += [total, swap(total, "row", n_row, 1)]
    factor = xor_blocks(factor, 1, n_col, col)
    factor = xor_blocks(factor, 0, n_col, col ^ (side * (n_col // 4)))
    whole = jnp.concatenate(panel)
    spread = dot(whole, factor, ((0,), (1,)))
    coeff = dot(check_weights(rows), spread)
    main = jnp.concatenate([part[:half] for part in summed])
    check = jnp.concatenate([part[half : half + sums.shape[0], :half] for part in summed], axis=1)
    updated = trailing - dot(spread, main)
    column_checks = (sums - dot(check, spread, ((1,), (1,)))).T
    row_checks = row_sums - dot(coeff, main)
    return (updated, column_checks, row_checks)


def solution(mesh):
    n_row, n_col = mesh.shape["row"], mesh.shape["col"]
    fits = n_col >= 4 and n_col & (n_col - 1) == 0 and n_row >= 2 and n_row & (n_row - 1) == 0

    def shards(*args):
        return steps(n_row, n_col, *args) if fits else plain(*args)

    placed = (P("row", "col"), P("row", "col"), P(), P("row", "col"), P("row", "col"))
    return jax.shard_map(
        shards,
        mesh=mesh,
        in_specs=placed,
        out_specs=(P("row", "col"), P("row", "col"), P("row", "col")),
        check_vma=False,
    )
```

```python
import jax
import jax.numpy as jnp
from jax import lax
from jax.experimental import pallas as pl
from jax.experimental.pallas import tpu as pltpu
from jax.sharding import PartitionSpec as P

EXTRA = 8
ORDERS = lambda b: (b, b[1:] + b[:1])
BLOCKS = (4, 2)
LOADS = 4
VMEM = 16777216
LIMIT = pltpu.CompilerParams(vmem_limit_bytes=VMEM)
ROWS = ((1,), (0,))
LANES = ((1,), (1,))


def dot(left, right, dims=ROWS):
    return lax.dot_general(left, right, (dims, ((), ())), precision=lax.Precision.HIGH, preferred_element_type=jnp.float32)


def once(left, right, dims=ROWS):
    return lax.dot_general(left, right, (dims, ((), ())), preferred_element_type=jnp.float32)


def high_low(value):
    high = value.astype(jnp.bfloat16)
    return high, (value - high.astype(jnp.float32)).astype(jnp.bfloat16)


def thrice(left, right, dims=ROWS):
    return once(left[0], right[0], dims) + (once(left[0], right[1], dims) + once(left[1], right[0], dims))


def swap(value, axis, size, distance):
    return lax.ppermute(value, axis, [(i, i ^ distance) for i in range(size)])


def swap_mixed(value, n_row, n_col, distances):
    pairs = [(r * n_col + c, (r ^ distances[c % 2]) * n_col + c) for r in range(n_row) for c in range(n_col)]
    return lax.ppermute(value, ("row", "col"), pairs)


def check_weights(count):
    local = jnp.arange(count).astype(jnp.float32)
    scale = 1.0 / jnp.sqrt(jnp.float32(count))
    return jnp.stack([jnp.ones((count,), jnp.float32) * scale, (local + 1.0) * scale / count])


def plain(trailing, reflectors, factor, column_sums, row_sums):
    panel = lax.all_gather(reflectors, "col", axis=1, tiled=True)
    columns = trailing.shape[1]
    joined = jnp.concatenate([trailing, column_sums], axis=1)
    image = dot(factor.T, lax.psum(dot(panel.T, joined), "row"))
    joined = joined - dot(panel, image)
    coeff = dot(check_weights(trailing.shape[0]), panel)
    return (joined[:, :columns], joined[:, columns:], row_sums - dot(coeff, image[:, :columns]))


def put(ref, product, check):
    half = product.shape[0]
    ref[:half, :] = product
    ref[half:, :] = jnp.zeros((EXTRA, ref.shape[1]), jnp.float32)
    ref[half:, :half] = check


def tall_sums(sums_ref):
    count, rows = sums_ref.shape
    return jnp.concatenate([sums_ref[...], jnp.zeros((EXTRA - count, rows), jnp.float32)], axis=0)


def next_kernel(high_ref, low_ref, sums_ref, *refs):
    panel = high_low(jnp.concatenate([ref[...] for ref in refs[:-1]], axis=0))
    product = thrice(panel, (high_ref[...], low_ref[...]))
    put(refs[-1], product, thrice(high_low(tall_sums(sums_ref)), panel, LANES))


def first_kernel(trailing_ref, piece_ref, sums_ref, out_ref, high_ref, low_ref, load_ref, panel_ref, check_ref, sems):
    rows = trailing_ref.shape[0]
    chunk = rows // LOADS
    loads = [pltpu.make_async_copy(piece_ref, panel_ref, sems.at[LOADS]), pltpu.make_async_copy(sums_ref, check_ref, sems.at[LOADS + 1])]
    for i in range(LOADS):
        band = pl.ds(i * chunk, chunk)
        loads.append(pltpu.make_async_copy(trailing_ref.at[band], load_ref.at[band], sems.at[i]))
    for load in loads:
        load.start()
    loads[0].wait()
    loads[1].wait()
    panel = high_low(panel_ref[...])
    check = thrice(high_low(tall_sums(check_ref)), panel, LANES)
    product = jnp.zeros((panel[0].shape[0], trailing_ref.shape[1]), jnp.float32)
    for i in range(LOADS):
        loads[2 + i].wait()
        band = slice(i * chunk, (i + 1) * chunk)
        part = high_low(load_ref[band, :])
        high_ref[band, :], low_ref[band, :] = part
        product += thrice((panel[0][:, band], panel[1][:, band]), part)
    put(out_ref, product, check)


VMEM_SPEC = pl.BlockSpec(memory_space=pltpu.VMEM)


def first_products(trailing, piece, sums):
    out = jax.ShapeDtypeStruct((piece.shape[0] + EXTRA, trailing.shape[1]), jnp.float32)
    part = jax.ShapeDtypeStruct(trailing.shape, jnp.bfloat16)
    return pl.pallas_call(
        first_kernel,
        in_specs=[pl.BlockSpec(memory_space=pltpu.HBM)] * 3,
        out_specs=[VMEM_SPEC] * 3,
        out_shape=[out, part, part],
        scratch_shapes=[pltpu.VMEM(a.shape, a.dtype) for a in (trailing, piece, sums)] + [pltpu.SemaphoreType.DMA((LOADS + 2,))],
        compiler_params=LIMIT,
    )(*[pltpu.with_memory_space_constraint(a, pltpu.HBM) for a in (trailing, piece, sums)])


def next_products(trailing, sums, pieces):
    half = sum(piece.shape[0] for piece in pieces)
    return pl.pallas_call(
        next_kernel,
        in_specs=[VMEM_SPEC] * (3 + len(pieces)),
        out_specs=VMEM_SPEC,
        out_shape=jax.ShapeDtypeStruct((half + EXTRA, trailing[0].shape[1]), jnp.float32),
        compiler_params=LIMIT,
    )(*trailing, sums, *pieces)


def spread_kernel(places_ref, order_ref, factor_ref, *refs):
    pieces, (high_ref, low_ref, late_ref, coeff_ref), (panel_ref, turned_ref) = refs[:-6], refs[-6:-2], refs[-2:]
    width = pieces[0].shape[0]
    for s, piece in enumerate(pieces):
        panel_ref[pl.ds(pl.multiple_of(places_ref[s], width), width), :] = piece[...]
        turned_ref[s * width : (s + 1) * width, :] = factor_ref[pl.ds(pl.multiple_of(order_ref[s], width), width), :]
    panel = jnp.transpose(panel_ref[...])
    spread = thrice(high_low(panel), high_low(turned_ref[...]), LANES)
    high, low = high_low(spread)
    high_ref[...] = high
    low_ref[...] = low
    size = panel.shape[1]
    late = size - late_ref.shape[1] // 4
    late_ref[...] = jnp.concatenate([high[:, late:], high[:, late:], low[:, late:], low[:, late:]], axis=1)
    count = panel.shape[0]
    scale = 1.0 / jnp.sqrt(jnp.float32(count))
    local = lax.broadcasted_iota(jnp.int32, (EXTRA, count), 1).astype(jnp.float32)
    kind = lax.broadcasted_iota(jnp.int32, (EXTRA, count), 0)
    weights = jnp.where(kind == 0, scale, jnp.where(kind == 1, (local + 1.0) * scale / count, 0.0))
    coeff_ref[...] = thrice(high_low(weights), (high, low))


def spreads(places, order, factor, pieces, late):
    size, rows = factor.shape[0], pieces[0].shape[1]
    return pl.pallas_call(
        spread_kernel,
        in_specs=[pl.BlockSpec(memory_space=pltpu.SMEM)] * 2 + [pl.BlockSpec(memory_space=pltpu.VMEM)] * (1 + len(pieces)),
        out_specs=[pl.BlockSpec(memory_space=pltpu.VMEM)] * 4,
        out_shape=[
            jax.ShapeDtypeStruct((rows, size), jnp.bfloat16),
            jax.ShapeDtypeStruct((rows, size), jnp.bfloat16),
            jax.ShapeDtypeStruct((rows, 4 * late), jnp.bfloat16),
            jax.ShapeDtypeStruct((EXTRA, size), jnp.float32),
        ],
        scratch_shapes=[pltpu.VMEM((size, rows), jnp.float32), pltpu.VMEM((size, size), jnp.float32)],
        compiler_params=LIMIT,
    )(places, order, factor, *pieces)


def apply_kernel(acc_ref, high_ref, low_ref, coeff_ref, rows_ref, sums_ref, *refs):
    parts, (out_ref, row_ref, col_ref) = refs[:-3], refs[-3:]
    tall = parts[0].shape[0] - EXTRA
    upto = tall * len(parts)
    right = high_low(jnp.concatenate([part[:tall, :] for part in parts], axis=0))
    left = (high_ref[:, :upto], low_ref[:, :upto])
    out_ref[...] = acc_ref[...] - thrice(left, right)
    check = jnp.concatenate([part[tall:, :tall] for part in parts], axis=1)
    col_ref[...] = sums_ref[...] - thrice(high_low(check), left, LANES)[: col_ref.shape[0]]

    @pl.when(pl.program_id(0) == 0)
    def _():
        row_ref[...] = rows_ref[...] - thrice(high_low(coeff_ref[:, :upto]), right)[: row_ref.shape[0]]


def finish_kernel(acc_ref, left_ref, coeff_ref, rows_ref, sums_ref, part_ref, out_ref, row_ref, col_ref):
    tall = part_ref.shape[0] - EXTRA
    high, low = high_low(part_ref[:tall, :])
    right = jnp.concatenate([high, low, high, low], axis=0)
    left = left_ref[...]
    out_ref[...] = acc_ref[...] - once(left, right)
    high, low = high_low(part_ref[tall:, :tall])
    col_ref[...] = sums_ref[...] - once(jnp.concatenate([high, low, high, low], axis=1), left, LANES)[: col_ref.shape[0]]

    @pl.when(pl.program_id(0) == 0)
    def _():
        size = coeff_ref.shape[1]
        high, low = high_low(coeff_ref[:, size - tall :])
        row_ref[...] = rows_ref[...] - once(jnp.concatenate([high, high, low, low], axis=1), right)[: row_ref.shape[0]]


def update(kernel, blocks, acc, lefts, coeff, row_sums, sums, parts):
    rows, _ = acc.shape
    tall = rows // blocks
    band = lambda array: pl.BlockSpec((tall, array.shape[1]), lambda i: (i, 0))
    whole = lambda array: pl.BlockSpec(array.shape, lambda i: (0,) * array.ndim)
    lanes = pl.BlockSpec((sums.shape[0], tall), lambda i: (0, i))
    return pl.pallas_call(
        kernel,
        grid=(blocks,),
        in_specs=[band(acc)] + [band(left) for left in lefts] + [whole(coeff), whole(row_sums), lanes] + [whole(part) for part in parts],
        out_specs=[band(acc), whole(row_sums), lanes],
        out_shape=[jax.ShapeDtypeStruct(a.shape, a.dtype) for a in (acc, row_sums, sums)],
        compiler_params=LIMIT,
    )(acc, *lefts, coeff, row_sums, sums, *parts)


def near(start, count, n_col):
    got = [start]
    for k in range(1, count):
        low = k & -k
        got.append(swap(got[k - low], "col", n_col, low))
    return got


def steps(n_row, n_col, trailing, reflectors, factor, column_sums, row_sums):
    width = reflectors.shape[1]
    row = lax.axis_index("row")
    col = lax.axis_index("col")
    half, quarter = n_col // 2, n_col // 4
    sums = column_sums.T
    bits = [1 << b for b in range(n_row.bit_length() - 1)]
    other = swap(reflectors.T, "col", n_col, half)
    mine = near(reflectors.T, half, n_col)
    own, high, low = first_products(trailing, mine[0], sums)
    others = near(other, half, n_col)
    summed = []
    order = []
    for g, pieces in enumerate((mine, others)):
        ways = list(zip(*ORDERS(bits)))
        side = jnp.where(col % 2 == 0, row // ways[0][0], row // ways[0][1]) % 2
        if g == 0 and quarter == 1:
            parts = [own]
        else:
            parts = [next_products((high, low), sums, pieces[:quarter])]
        parts.append(next_products((high, low), sums, pieces[quarter:]))
        total = jnp.where(side == 0, parts[0], parts[1])
        value = jnp.where(side == 0, parts[1], parts[0])
        for way in ways:
            total = total + swap_mixed(value, n_row, n_col, way)
            value = total
        summed += [total, swap_mixed(total, n_row, n_col, ways[0])]
        order.append((jnp.arange(half) + g * half) ^ col ^ (side * quarter))
    places = (jnp.arange(n_col) ^ col) * width
    order = jnp.concatenate(order) * width
    late = quarter * width
    high, low, last, coeff = spreads(places, order, factor, mine + others, late)
    acc, row_sums, sums = update(apply_kernel, BLOCKS[0], trailing, (high, low), coeff, row_sums, sums, summed[:-1])
    updated, row_checks, sums = update(finish_kernel, BLOCKS[1], acc, (last,), coeff, row_sums, sums, summed[-1:])
    return (updated, sums.T, row_checks)


def solution(mesh):
    n_row, n_col = mesh.shape["row"], mesh.shape["col"]
    fits = n_col >= 4 and n_col & (n_col - 1) == 0 and n_row >= 2 and n_row & (n_row - 1) == 0

    def shards(*args):
        return steps(n_row, n_col, *args) if fits else plain(*args)

    placed = (P("row", "col"), P("row", "col"), P(), P("row", "col"), P("row", "col"))
    return jax.shard_map(
        shards,
        mesh=mesh,
        in_specs=placed,
        out_specs=(P("row", "col"), P("row", "col"), P("row", "col")),
        check_vma=False,
    )
```

```python
import jax
import jax.numpy as jnp
from jax import lax
from jax.experimental import pallas as pl
from jax.experimental.pallas import tpu as pltpu
from jax.sharding import PartitionSpec as P

EXTRA = 8
LANE = 128
LOADS = 4
STORES = 4
VMEM = 16 << 20
LIMIT = pltpu.CompilerParams(vmem_limit_bytes=VMEM)
ROWS = ((1,), (0,))
LANES = ((1,), (1,))


def dot(left, right, dims=ROWS):
    return lax.dot_general(left, right, (dims, ((), ())), precision=lax.Precision.HIGH, preferred_element_type=jnp.float32)


def once(left, right, dims=ROWS):
    return lax.dot_general(left, right, (dims, ((), ())), preferred_element_type=jnp.float32)


def high_low(value):
    high = value.astype(jnp.bfloat16)
    return high, (value - high.astype(jnp.float32)).astype(jnp.bfloat16)


def thrice(left, right, dims=ROWS):
    return once(left[0], right[0], dims) + (once(left[0], right[1], dims) + once(left[1], right[0], dims))


def stacked(left, right, dims=ROWS):
    count = left[0].shape[0]
    both = once(jnp.concatenate(left, axis=0), right[0], dims)
    return both[:count] + (both[count:] + once(left[0], right[1], dims))


def swap(value, axis, size, distance):
    return lax.ppermute(value, axis, [(i, i ^ distance) for i in range(size)])


def swap_mixed(value, n_row, n_col, distances):
    pairs = [(r * n_col + c, (r ^ distances[c % 2]) * n_col + c) for r in range(n_row) for c in range(n_col)]
    return lax.ppermute(value, ("row", "col"), pairs)


def check_weights(count):
    local = jnp.arange(count).astype(jnp.float32)
    scale = 1.0 / jnp.sqrt(jnp.float32(count))
    return jnp.stack([jnp.ones((count,), jnp.float32) * scale, (local + 1.0) * scale / count])


def plain(trailing, reflectors, factor, column_sums, row_sums):
    panel = lax.all_gather(reflectors, "col", axis=1, tiled=True)
    columns = trailing.shape[1]
    joined = jnp.concatenate([trailing, column_sums], axis=1)
    image = dot(factor.T, lax.psum(dot(panel.T, joined), "row"))
    joined = joined - dot(panel, image)
    coeff = dot(check_weights(trailing.shape[0]), panel)
    return (joined[:, :columns], joined[:, columns:], row_sums - dot(coeff, image[:, :columns]))


def put(ref, product, check):
    half, columns = product.shape
    for t in range(columns // LANE):
        ref[t * half : (t + 1) * half, :] = product[:, t * LANE : (t + 1) * LANE]
    end = columns // LANE * half
    ref[end:, :] = jnp.zeros((EXTRA, LANE), jnp.float32)
    ref[end:, :half] = check


def packed(half, columns):
    return jax.ShapeDtypeStruct((columns // LANE * half + EXTRA, LANE), jnp.float32)


def take(ref, columns):
    tiles = columns // LANE
    half = (ref.shape[0] - EXTRA) // tiles
    product = jnp.concatenate([ref[t * half : (t + 1) * half, :] for t in range(tiles)], axis=1)
    return product, ref[tiles * half :, :half]


def tall_sums(sums_ref):
    count, rows = sums_ref.shape
    return jnp.concatenate([sums_ref[...], jnp.zeros((EXTRA - count, rows), jnp.float32)], axis=0)


def next_kernel(high_ref, low_ref, sums_ref, *refs):
    panel = high_low(jnp.concatenate([ref[...] for ref in refs[:-1]], axis=0))
    product = stacked(panel, (high_ref[...], low_ref[...]))
    put(refs[-1], product, thrice(high_low(tall_sums(sums_ref)), panel, LANES))


def first_kernel(trailing_ref, piece_ref, sums_ref, out_ref, high_ref, low_ref, load_ref, panel_ref, check_ref, sems):
    rows = trailing_ref.shape[0]
    chunk = rows // LOADS
    loads = [pltpu.make_async_copy(piece_ref, panel_ref, sems.at[LOADS]), pltpu.make_async_copy(sums_ref, check_ref, sems.at[LOADS + 1])]
    for i in range(LOADS):
        band = pl.ds(i * chunk, chunk)
        loads.append(pltpu.make_async_copy(trailing_ref.at[band], load_ref.at[band], sems.at[i]))
    for load in loads:
        load.start()
    loads[0].wait()
    loads[1].wait()
    panel = high_low(panel_ref[...])
    check = thrice(high_low(tall_sums(check_ref)), panel, LANES)
    product = jnp.zeros((panel[0].shape[0], trailing_ref.shape[1]), jnp.float32)
    for i in range(LOADS):
        loads[2 + i].wait()
        band = slice(i * chunk, (i + 1) * chunk)
        part = high_low(load_ref[band, :])
        high_ref[band, :], low_ref[band, :] = part
        product += stacked((panel[0][:, band], panel[1][:, band]), part)
    put(out_ref, product, check)


VMEM_SPEC = pl.BlockSpec(memory_space=pltpu.VMEM)


def first_products(trailing, piece, sums):
    out = packed(piece.shape[0], trailing.shape[1])
    part = jax.ShapeDtypeStruct(trailing.shape, jnp.bfloat16)
    return pl.pallas_call(
        first_kernel,
        in_specs=[pl.BlockSpec(memory_space=pltpu.HBM)] * 3,
        out_specs=[VMEM_SPEC] * 3,
        out_shape=[out, part, part],
        scratch_shapes=[pltpu.VMEM(a.shape, a.dtype) for a in (trailing, piece, sums)] + [pltpu.SemaphoreType.DMA((LOADS + 2,))],
        compiler_params=LIMIT,
    )(*[pltpu.with_memory_space_constraint(a, pltpu.HBM) for a in (trailing, piece, sums)])


def next_products(trailing, sums, pieces):
    half = sum(piece.shape[0] for piece in pieces)
    return pl.pallas_call(
        next_kernel,
        in_specs=[VMEM_SPEC] * (3 + len(pieces)),
        out_specs=VMEM_SPEC,
        out_shape=packed(half, trailing[0].shape[1]),
        compiler_params=LIMIT,
    )(*trailing, sums, *pieces)


def spread_kernel(places_ref, order_ref, factor_ref, *refs):
    pieces, (high_ref, low_ref, late_ref, coeff_ref), (panel_ref, turned_ref) = refs[:-6], refs[-6:-2], refs[-2:]
    width = pieces[0].shape[0]
    for s, piece in enumerate(pieces):
        panel_ref[pl.ds(pl.multiple_of(places_ref[s], width), width), :] = piece[...]
        turned_ref[s * width : (s + 1) * width, :] = factor_ref[pl.ds(pl.multiple_of(order_ref[s], width), width), :]
    panel = jnp.transpose(panel_ref[...])
    spread = thrice(high_low(panel), high_low(turned_ref[...]), LANES)
    high, low = high_low(spread)
    high_ref[...] = high
    low_ref[...] = low
    size = panel.shape[1]
    late = size - late_ref.shape[1] // 4
    late_ref[...] = jnp.concatenate([high[:, late:], high[:, late:], low[:, late:], low[:, late:]], axis=1)
    count = panel.shape[0]
    scale = 1.0 / jnp.sqrt(jnp.float32(count))
    local = lax.broadcasted_iota(jnp.int32, (EXTRA, count), 1).astype(jnp.float32)
    kind = lax.broadcasted_iota(jnp.int32, (EXTRA, count), 0)
    weights = jnp.where(kind == 0, scale, jnp.where(kind == 1, (local + 1.0) * scale / count, 0.0))
    coeff_ref[...] = thrice(high_low(weights), (high, low))


def spreads(places, order, factor, pieces, late):
    size, rows = factor.shape[0], pieces[0].shape[1]
    return pl.pallas_call(
        spread_kernel,
        in_specs=[pl.BlockSpec(memory_space=pltpu.SMEM)] * 2 + [pl.BlockSpec(memory_space=pltpu.VMEM)] * (1 + len(pieces)),
        out_specs=[pl.BlockSpec(memory_space=pltpu.VMEM)] * 4,
        out_shape=[
            jax.ShapeDtypeStruct((rows, size), jnp.bfloat16),
            jax.ShapeDtypeStruct((rows, size), jnp.bfloat16),
            jax.ShapeDtypeStruct((rows, 4 * late), jnp.bfloat16),
            jax.ShapeDtypeStruct((EXTRA, size), jnp.float32),
        ],
        scratch_shapes=[pltpu.VMEM((size, rows), jnp.float32), pltpu.VMEM((size, size), jnp.float32)],
        compiler_params=LIMIT,
    )(places, order, factor, *pieces)


def apply_kernel(acc_ref, high_ref, low_ref, coeff_ref, rows_ref, sums_ref, *refs):
    parts, (out_ref, row_ref, col_ref), (load_ref, sems) = refs[:-5], refs[-5:-2], refs[-2:]
    rows, columns = acc_ref.shape
    chunk = rows // LOADS
    bands = [pl.ds(i * chunk, chunk) for i in range(LOADS)]
    loads = [pltpu.make_async_copy(acc_ref.at[band], load_ref.at[band], sems.at[i]) for i, band in enumerate(bands)]
    for load in loads:
        load.start()
    took = [take(part, columns) for part in parts]
    right = high_low(jnp.concatenate([product for product, _ in took], axis=0))
    upto = right[0].shape[0]
    check = jnp.concatenate([check for _, check in took], axis=1)
    left = (high_ref[:, :upto], low_ref[:, :upto])
    row_ref[...] = rows_ref[...] - thrice(high_low(coeff_ref[:, :upto]), right)[: row_ref.shape[0]]
    col_ref[...] = sums_ref[...] - thrice(high_low(check), left, LANES)[: col_ref.shape[0]]
    for band, load in zip(bands, loads):
        some = thrice((high_ref[band, :upto], low_ref[band, :upto]), right)
        load.wait()
        out_ref[band, :] = load_ref[band, :] - some


def applied(acc, high, low, coeff, row_sums, sums, parts):
    return pl.pallas_call(
        apply_kernel,
        in_specs=[pl.BlockSpec(memory_space=pltpu.HBM)] + [VMEM_SPEC] * (5 + len(parts)),
        out_specs=[VMEM_SPEC] * 3,
        out_shape=[jax.ShapeDtypeStruct(a.shape, a.dtype) for a in (acc, row_sums, sums)],
        scratch_shapes=[pltpu.VMEM(acc.shape, acc.dtype), pltpu.SemaphoreType.DMA((LOADS,))],
        compiler_params=LIMIT,
    )(pltpu.with_memory_space_constraint(acc, pltpu.HBM), high, low, coeff, row_sums, sums, *parts)


def finish_kernel(acc_ref, left_ref, coeff_ref, rows_ref, sums_ref, part_ref, out_ref, row_ref, col_ref, done_ref, row_done, col_done, sems):
    rows, columns = acc_ref.shape
    product, check = take(part_ref, columns)
    high, low = high_low(product)
    right = jnp.concatenate([high, low, high, low], axis=0)
    chunk = rows // STORES
    stores = []
    for i in range(STORES):
        band = pl.ds(i * chunk, chunk)
        done_ref[band, :] = acc_ref[band, :] - once(left_ref[band, :], right)
        stores.append(pltpu.make_async_copy(done_ref.at[band], out_ref.at[band], sems.at[i]))
        stores[-1].start()
    high, low = high_low(check)
    col_done[...] = sums_ref[...] - once(jnp.concatenate([high, low, high, low], axis=1), left_ref[...], LANES)[: col_ref.shape[0]]
    stores.append(pltpu.make_async_copy(col_done, col_ref, sems.at[STORES]))
    stores[-1].start()
    high, low = high_low(coeff_ref[:, coeff_ref.shape[1] - product.shape[0] :])
    row_done[...] = rows_ref[...] - once(jnp.concatenate([high, high, low, low], axis=1), right)[: row_ref.shape[0]]
    stores.append(pltpu.make_async_copy(row_done, row_ref, sems.at[STORES + 1]))
    stores[-1].start()
    for store in stores:
        store.wait()


def finished(acc, left, coeff, row_sums, sums, part):
    outs = (acc, row_sums, sums)
    return pl.pallas_call(
        finish_kernel,
        in_specs=[VMEM_SPEC] * 6,
        out_specs=[pl.BlockSpec(memory_space=pltpu.HBM)] * 3,
        out_shape=[jax.ShapeDtypeStruct(a.shape, a.dtype) for a in outs],
        scratch_shapes=[pltpu.VMEM(a.shape, a.dtype) for a in outs] + [pltpu.SemaphoreType.DMA((STORES + 2,))],
        compiler_params=LIMIT,
    )(acc, left, coeff, row_sums, sums, part)


def near(start, count, n_col):
    got = [start]
    for k in range(1, count):
        low = k & -k
        got.append(swap(got[k - low], "col", n_col, low))
    return got


def steps(n_row, n_col, trailing, reflectors, factor, column_sums, row_sums):
    width = reflectors.shape[1]
    row = lax.axis_index("row")
    col = lax.axis_index("col")
    half, quarter = n_col // 2, n_col // 4
    sums = column_sums.T
    bits = [1 << b for b in range(n_row.bit_length() - 1)]
    other = swap(reflectors.T, "col", n_col, half)
    mine = near(reflectors.T, half, n_col)
    own, high, low = first_products(trailing, mine[0], sums)
    others = near(other, half, n_col)
    summed = []
    order = []
    for g, pieces in enumerate((mine, others)):
        ways = list(zip(bits, bits[1:] + bits[:1]))
        side = jnp.where(col % 2 == 0, row // ways[0][0], row // ways[0][1]) % 2
        if g == 0 and quarter == 1:
            parts = [own]
        else:
            parts = [next_products((high, low), sums, pieces[:quarter])]
        parts.append(next_products((high, low), sums, pieces[quarter:]))
        total = jnp.where(side == 0, parts[0], parts[1])
        value = jnp.where(side == 0, parts[1], parts[0])
        for way in ways:
            total = total + swap_mixed(value, n_row, n_col, way)
            value = total
        summed += [total, swap_mixed(total, n_row, n_col, ways[0])]
        order.append((jnp.arange(half) + g * half) ^ col ^ (side * quarter))
    places = (jnp.arange(n_col) ^ col) * width
    order = jnp.concatenate(order) * width
    late = quarter * width
    high, low, last, coeff = spreads(places, order, factor, mine + others, late)
    acc, row_sums, sums = applied(trailing, high, low, coeff, row_sums, sums, summed[:-1])
    updated, row_checks, sums = finished(acc, last, coeff, row_sums, sums, summed[-1])
    return (updated, sums.T, row_checks)


def solution(mesh):
    n_row, n_col = mesh.shape["row"], mesh.shape["col"]
    fits = n_col >= 4 and n_col & (n_col - 1) == 0 and n_row >= 2 and n_row & (n_row - 1) == 0

    def shards(*args):
        return steps(n_row, n_col, *args) if fits else plain(*args)

    placed = (P("row", "col"), P("row", "col"), P(), P("row", "col"), P("row", "col"))
    return jax.shard_map(
        shards,
        mesh=mesh,
        in_specs=placed,
        out_specs=(P("row", "col"), P("row", "col"), P("row", "col")),
        check_vma=False,
    )
```

```python
import jax
import jax.numpy as jnp
from jax import lax
from jax.experimental import pallas as pl
from jax.experimental.pallas import tpu as pltpu
from jax.sharding import PartitionSpec as P

EXTRA = 8
LANE = 128
LOADS = 4
STORES = 8
VMEM = 16 << 20
LIMIT = pltpu.CompilerParams(vmem_limit_bytes=VMEM)
ROWS = ((1,), (0,))
LANES = ((1,), (1,))


def dot(left, right, dims=ROWS):
    return lax.dot_general(left, right, (dims, ((), ())), precision=lax.Precision.HIGH, preferred_element_type=jnp.float32)


def once(left, right, dims=ROWS):
    return lax.dot_general(left, right, (dims, ((), ())), preferred_element_type=jnp.float32)


def high_low(value):
    high = value.astype(jnp.bfloat16)
    return high, (value - high.astype(jnp.float32)).astype(jnp.bfloat16)


def thrice(left, right, dims=ROWS):
    return once(left[0], right[0], dims) + (once(left[0], right[1], dims) + once(left[1], right[0], dims))


def stacked(left, right, dims=ROWS):
    count = left[0].shape[0]
    both = once(jnp.concatenate(left, axis=0), right[0], dims)
    return both[:count] + (both[count:] + once(left[0], right[1], dims))


def swap(value, axis, size, distance):
    return lax.ppermute(value, axis, [(i, i ^ distance) for i in range(size)])


def swap_mixed(value, n_row, n_col, distances):
    pairs = [(r * n_col + c, (r ^ distances[c % 2]) * n_col + c) for r in range(n_row) for c in range(n_col)]
    return lax.ppermute(value, ("row", "col"), pairs)


def check_weights(count):
    local = jnp.arange(count).astype(jnp.float32)
    scale = 1.0 / jnp.sqrt(jnp.float32(count))
    return jnp.stack([jnp.ones((count,), jnp.float32) * scale, (local + 1.0) * scale / count])


def plain(trailing, reflectors, factor, column_sums, row_sums):
    panel = lax.all_gather(reflectors, "col", axis=1, tiled=True)
    columns = trailing.shape[1]
    joined = jnp.concatenate([trailing, column_sums], axis=1)
    image = dot(factor.T, lax.psum(dot(panel.T, joined), "row"))
    joined = joined - dot(panel, image)
    coeff = dot(check_weights(trailing.shape[0]), panel)
    return (joined[:, :columns], joined[:, columns:], row_sums - dot(coeff, image[:, :columns]))


def put(ref, product, check):
    half, columns = product.shape
    for t in range(columns // LANE):
        ref[t * half : (t + 1) * half, :] = product[:, t * LANE : (t + 1) * LANE]
    end = columns // LANE * half
    ref[end:, :] = jnp.zeros((EXTRA, LANE), jnp.float32)
    ref[end:, :half] = check


def packed(half, columns):
    return jax.ShapeDtypeStruct((columns // LANE * half + EXTRA, LANE), jnp.float32)


def take(ref, columns):
    tiles = columns // LANE
    half = (ref.shape[0] - EXTRA) // tiles
    product = jnp.concatenate([ref[t * half : (t + 1) * half, :] for t in range(tiles)], axis=1)
    return product, ref[tiles * half :, :half]


def split_check(product, columns):
    return product[:, :columns], jnp.transpose(product[:, columns:])[:EXTRA]


def next_kernel(high_ref, low_ref, *refs):
    panel = high_low(jnp.concatenate([ref[...] for ref in refs[:-1]], axis=0))
    product = stacked(panel, (high_ref[...], low_ref[...]))
    put(refs[-1], *split_check(product, high_ref.shape[1] - LANE))


def first_kernel(trailing_ref, piece_ref, sums_ref, out_ref, high_ref, low_ref, load_ref, panel_ref, check_ref, sems):
    rows = trailing_ref.shape[0]
    chunk = rows // LOADS
    loads = [pltpu.make_async_copy(piece_ref, panel_ref, sems.at[LOADS]), pltpu.make_async_copy(sums_ref, check_ref, sems.at[LOADS + 1])]
    for i in range(LOADS):
        band = pl.ds(i * chunk, chunk)
        loads.append(pltpu.make_async_copy(trailing_ref.at[band], load_ref.at[band], sems.at[i]))
    for load in loads:
        load.start()
    loads[0].wait()
    loads[1].wait()
    panel = high_low(panel_ref[...])
    columns = trailing_ref.shape[1]
    sums = jnp.transpose(jnp.concatenate([check_ref[...], jnp.zeros((LANE - check_ref.shape[0], rows), jnp.float32)], axis=0))
    high_ref[:, columns:], low_ref[:, columns:] = high_low(sums)
    product = jnp.zeros((panel[0].shape[0], columns + LANE), jnp.float32)
    for i in range(LOADS):
        loads[2 + i].wait()
        band = slice(i * chunk, (i + 1) * chunk)
        high_ref[band, :columns], low_ref[band, :columns] = high_low(load_ref[band, :])
        product += stacked((panel[0][:, band], panel[1][:, band]), (high_ref[band, :], low_ref[band, :]))
    put(out_ref, *split_check(product, columns))


VMEM_SPEC = pl.BlockSpec(memory_space=pltpu.VMEM)


def first_products(trailing, piece, sums):
    out = packed(piece.shape[0], trailing.shape[1])
    part = jax.ShapeDtypeStruct((trailing.shape[0], trailing.shape[1] + LANE), jnp.bfloat16)
    return pl.pallas_call(
        first_kernel,
        in_specs=[pl.BlockSpec(memory_space=pltpu.HBM)] * 3,
        out_specs=[VMEM_SPEC] * 3,
        out_shape=[out, part, part],
        scratch_shapes=[pltpu.VMEM(a.shape, a.dtype) for a in (trailing, piece, sums)] + [pltpu.SemaphoreType.DMA((LOADS + 2,))],
        compiler_params=LIMIT,
    )(*[pltpu.with_memory_space_constraint(a, pltpu.HBM) for a in (trailing, piece, sums)])


def next_products(trailing, pieces):
    half = sum(piece.shape[0] for piece in pieces)
    return pl.pallas_call(
        next_kernel,
        in_specs=[VMEM_SPEC] * (2 + len(pieces)),
        out_specs=VMEM_SPEC,
        out_shape=packed(half, trailing[0].shape[1] - LANE),
        compiler_params=LIMIT,
    )(*trailing, *pieces)


def spread_kernel(places_ref, order_ref, factor_ref, *refs):
    pieces, (high_ref, low_ref, late_ref, coeff_ref), (panel_ref, turned_ref) = refs[:-6], refs[-6:-2], refs[-2:]
    width = pieces[0].shape[0]
    for s, piece in enumerate(pieces):
        panel_ref[pl.ds(pl.multiple_of(places_ref[s], width), width), :] = piece[...]
        turned_ref[s * width : (s + 1) * width, :] = factor_ref[pl.ds(pl.multiple_of(order_ref[s], width), width), :]
    panel = jnp.transpose(panel_ref[...])
    spread = thrice(high_low(panel), high_low(turned_ref[...]), LANES)
    high, low = high_low(spread)
    high_ref[...] = high
    low_ref[...] = low
    size = panel.shape[1]
    late = size - late_ref.shape[1] // 4
    late_ref[...] = jnp.concatenate([high[:, late:], high[:, late:], low[:, late:], low[:, late:]], axis=1)
    count = panel.shape[0]
    scale = 1.0 / jnp.sqrt(jnp.float32(count))
    local = lax.broadcasted_iota(jnp.int32, (EXTRA, count), 1).astype(jnp.float32)
    kind = lax.broadcasted_iota(jnp.int32, (EXTRA, count), 0)
    weights = jnp.where(kind == 0, scale, jnp.where(kind == 1, (local + 1.0) * scale / count, 0.0))
    coeff_ref[...] = thrice(high_low(weights), (high, low))


def spreads(places, order, factor, pieces, late):
    size, rows = factor.shape[0], pieces[0].shape[1]
    return pl.pallas_call(
        spread_kernel,
        in_specs=[pl.BlockSpec(memory_space=pltpu.SMEM)] * 2 + [pl.BlockSpec(memory_space=pltpu.VMEM)] * (1 + len(pieces)),
        out_specs=[pl.BlockSpec(memory_space=pltpu.VMEM)] * 4,
        out_shape=[
            jax.ShapeDtypeStruct((rows, size), jnp.bfloat16),
            jax.ShapeDtypeStruct((rows, size), jnp.bfloat16),
            jax.ShapeDtypeStruct((rows, 4 * late), jnp.bfloat16),
            jax.ShapeDtypeStruct((EXTRA, size), jnp.float32),
        ],
        scratch_shapes=[pltpu.VMEM((size, rows), jnp.float32), pltpu.VMEM((size, size), jnp.float32)],
        compiler_params=LIMIT,
    )(places, order, factor, *pieces)


def apply_kernel(acc_ref, high_ref, low_ref, coeff_ref, rows_ref, sums_ref, *refs):
    parts, (out_ref, row_ref, col_ref), (load_ref, sems) = refs[:-5], refs[-5:-2], refs[-2:]
    rows, columns = acc_ref.shape
    chunk = rows // LOADS
    bands = [pl.ds(i * chunk, chunk) for i in range(LOADS)]
    loads = [pltpu.make_async_copy(acc_ref.at[band], load_ref.at[band], sems.at[i]) for i, band in enumerate(bands)]
    for load in loads:
        load.start()
    took = [take(part, columns) for part in parts]
    right = high_low(jnp.concatenate([product for product, _ in took], axis=0))
    upto = right[0].shape[0]
    check = jnp.concatenate([check for _, check in took], axis=1)
    left = (high_ref[:, :upto], low_ref[:, :upto])
    row_ref[...] = rows_ref[...] - thrice(high_low(coeff_ref[:, :upto]), right)[: row_ref.shape[0]]
    col_ref[...] = sums_ref[...] - thrice(high_low(check), left, LANES)[: col_ref.shape[0]]
    for band, load in zip(bands, loads):
        some = thrice((high_ref[band, :upto], low_ref[band, :upto]), right)
        load.wait()
        out_ref[band, :] = load_ref[band, :] - some


def applied(acc, high, low, coeff, row_sums, sums, parts):
    return pl.pallas_call(
        apply_kernel,
        in_specs=[pl.BlockSpec(memory_space=pltpu.HBM)] + [VMEM_SPEC] * (5 + len(parts)),
        out_specs=[VMEM_SPEC] * 3,
        out_shape=[jax.ShapeDtypeStruct(a.shape, a.dtype) for a in (acc, row_sums, sums)],
        scratch_shapes=[pltpu.VMEM(acc.shape, acc.dtype), pltpu.SemaphoreType.DMA((LOADS,))],
        compiler_params=LIMIT,
    )(pltpu.with_memory_space_constraint(acc, pltpu.HBM), high, low, coeff, row_sums, sums, *parts)


def finish_kernel(acc_ref, left_ref, coeff_ref, rows_ref, sums_ref, part_ref, out_ref, row_ref, col_ref, done_ref, row_done, col_done, sems):
    rows, columns = acc_ref.shape
    product, check = take(part_ref, columns)
    high, low = high_low(product)
    right = jnp.concatenate([high, low, high, low], axis=0)
    chunk = rows // STORES
    stores = []
    for i in range(STORES):
        band = pl.ds(i * chunk, chunk)
        done_ref[band, :] = acc_ref[band, :] - once(left_ref[band, :], right)
        stores.append(pltpu.make_async_copy(done_ref.at[band], out_ref.at[band], sems.at[i]))
        stores[-1].start()
    high, low = high_low(check)
    col_done[...] = sums_ref[...] - once(jnp.concatenate([high, low, high, low], axis=1), left_ref[...], LANES)[: col_ref.shape[0]]
    stores.append(pltpu.make_async_copy(col_done, col_ref, sems.at[STORES]))
    stores[-1].start()
    high, low = high_low(coeff_ref[:, coeff_ref.shape[1] - product.shape[0] :])
    row_done[...] = rows_ref[...] - once(jnp.concatenate([high, high, low, low], axis=1), right)[: row_ref.shape[0]]
    stores.append(pltpu.make_async_copy(row_done, row_ref, sems.at[STORES + 1]))
    stores[-1].start()
    for store in stores:
        store.wait()


def finished(acc, left, coeff, row_sums, sums, part):
    outs = (acc, row_sums, sums)
    return pl.pallas_call(
        finish_kernel,
        in_specs=[VMEM_SPEC] * 6,
        out_specs=[pl.BlockSpec(memory_space=pltpu.HBM)] * 3,
        out_shape=[jax.ShapeDtypeStruct(a.shape, a.dtype) for a in outs],
        scratch_shapes=[pltpu.VMEM(a.shape, a.dtype) for a in outs] + [pltpu.SemaphoreType.DMA((STORES + 2,))],
        compiler_params=LIMIT,
    )(acc, left, coeff, row_sums, sums, part)


def near(start, count, n_col):
    got = [start]
    for k in range(1, count):
        low = k & -k
        got.append(swap(got[k - low], "col", n_col, low))
    return got


def steps(n_row, n_col, trailing, reflectors, factor, column_sums, row_sums):
    width = reflectors.shape[1]
    row = lax.axis_index("row")
    col = lax.axis_index("col")
    half, quarter = n_col // 2, n_col // 4
    sums = column_sums.T
    bits = [1 << b for b in range(n_row.bit_length() - 1)]
    other = swap(reflectors.T, "col", n_col, half)
    mine = near(reflectors.T, half, n_col)
    own, high, low = first_products(trailing, mine[0], sums)
    others = near(other, half, n_col)
    summed = []
    order = []
    for g, pieces in enumerate((mine, others)):
        ways = list(zip(bits, bits[1:] + bits[:1]))
        side = jnp.where(col % 2 == 0, row // ways[0][0], row // ways[0][1]) % 2
        if g == 0 and quarter == 1:
            parts = [own]
        else:
            parts = [next_products((high, low), pieces[:quarter])]
        parts.append(next_products((high, low), pieces[quarter:]))
        total = jnp.where(side == 0, parts[0], parts[1])
        value = jnp.where(side == 0, parts[1], parts[0])
        for way in ways:
            total = total + swap_mixed(value, n_row, n_col, way)
            value = total
        summed += [total, swap_mixed(total, n_row, n_col, ways[0])]
        order.append((jnp.arange(half) + g * half) ^ col ^ (side * quarter))
    places = (jnp.arange(n_col) ^ col) * width
    order = jnp.concatenate(order) * width
    late = quarter * width
    high, low, last, coeff = spreads(places, order, factor, mine + others, late)
    acc, row_sums, sums = applied(trailing, high, low, coeff, row_sums, sums, summed[:-1])
    updated, row_checks, sums = finished(acc, last, coeff, row_sums, sums, summed[-1])
    return (updated, sums.T, row_checks)


def solution(mesh):
    n_row, n_col = mesh.shape["row"], mesh.shape["col"]
    fits = n_col >= 4 and n_col & (n_col - 1) == 0 and n_row >= 2 and n_row & (n_row - 1) == 0

    def shards(*args):
        return steps(n_row, n_col, *args) if fits else plain(*args)

    placed = (P("row", "col"), P("row", "col"), P(), P("row", "col"), P("row", "col"))
    return jax.shard_map(
        shards,
        mesh=mesh,
        in_specs=placed,
        out_specs=(P("row", "col"), P("row", "col"), P("row", "col")),
        check_vma=False,
    )
```
